32 devices in a mesh: dp: 16 (over z, x, core), mp: 2 (over y).
Axes of the slice: x: 2, y: 2, z: 4, core: 2. Of those that a mesh axis runs over, the one named last changes fastest.
Arguments:
- activations: bfloat16 [2, 2048, 3968], P(None, 'dp'), may hold values from -6 to 6
- out_grads: bfloat16 [2, 2048, 992], P(None, 'dp', 'mp'), may hold values from -0.29882812 to 0.29882812
- error_memory: bfloat16 [63488, 992], P('dp', 'mp'), may hold values from -6 to 6
- q_previous: float32 [992, 32], P('mp'), may hold values from -6 to 6
Outputs:
- new_error: bfloat16 [63488, 992], P('dp', 'mp')
- p_basis: float32 [3968, 32], P('dp')
- q_factor: float32 [992, 32], P('mp')
The draws below stay inside these ranges and needn't reach their ends.
All inputs are finite; a program needn't handle non-finite values.
Results may differ from the reference program's by a relative error of at most 0.001.
Values sent between devices are 32-bit elements; how exact they have to be, the bound alone decides.
No kernel may reach another device: no remote copies, remote signals or barrier semaphores. Data moves between devices by JAX's collectives and lax.ppermute only.
A program may use at most 64 MiB of HBM per device.

```python
import jax
import jax.numpy as jnp
from jax import lax

D = 3968
R = 32
MICRO = 2
TOK_DEV = 128
TOKENS = 2048
F = 992
ERR_ROWS = 63488
N_DP = 16


def levels(stream_key, shape, split, smallest, top_value):
    level = 1.0
    for position, blocks in split:
        heights = jax.random.uniform(jax.random.fold_in(jax.random.fold_in(stream_key, 6), position), (blocks,), jnp.float32, smallest / len(split), top_value / len(split))
        level = level * jnp.repeat(jnp.exp(heights), shape[position] // blocks).reshape((-1,) + (1,) * (len(shape) - 1 - position))
    return level


def scatter_about(own_key, shape, deviation, limit, cuts=(), dtype=jnp.bfloat16):
    drawn = jax.random.normal(own_key, shape, jnp.float32) * deviation
    if len(cuts) > 0:
        drawn = levels(own_key, shape, cuts, -0.22, 0.18) * drawn
    return jnp.clip(drawn, min=-limit, max=limit).astype(dtype)


def setup_inputs(seed: int = 0) -> dict:
    splits = jax.random.split(jax.random.key(seed), 5)
    return {
        "activations": scatter_about(splits[0], (MICRO, TOKENS, D), 1.0, 6.0, ((1, 16),)),
        "out_grads": scatter_about(splits[1], (MICRO, TOKENS, F), 0.044, 0.29882812, ((1, 16), (2, 2))),
        "error_memory": scatter_about(splits[2], (ERR_ROWS, F), 1.0, 6.0, ((0, 16), (1, 2))),
        "q_previous": scatter_about(splits[3], (F, R), 1.0, 6.0, ((0, 2),), jnp.float32),
    }


def reference(activations, out_grads, error_memory, q_previous):
    acts_all = activations.reshape(MICRO, N_DP, TOK_DEV, D).transpose(1, 0, 2, 3).reshape(N_DP, MICRO * TOK_DEV, D)
    grads_all = out_grads.reshape(MICRO, N_DP, TOK_DEV, F).transpose(1, 0, 2, 3).reshape(N_DP, MICRO * TOK_DEV, F)
    errors_all = error_memory.reshape(N_DP, D, F)

    def form_merged(items):
        token_rows, grad_rows, memory = items
        product = jnp.einsum('td,tf->df', token_rows.astype(jnp.float32), grad_rows.astype(jnp.float32), preferred_element_type=jnp.float32)
        return product + memory.astype(jnp.float32)
    merged_all = lax.map(form_merged, (acts_all, grads_all, errors_all))
    p_whole = jnp.einsum('idf,fr->dr', merged_all, q_previous, precision=lax.Precision.HIGHEST)
    gram_total = jnp.dot(p_whole.T, p_whole, precision=lax.Precision.HIGHEST)
    lower_factor = jnp.linalg.cholesky(gram_total)
    p_basis = jax.scipy.linalg.solve_triangular(lower_factor, p_whole.T, lower=True).T
    q_factor = jnp.einsum('idf,dr->fr', merged_all, p_basis, precision=lax.Precision.HIGHEST) / N_DP
    approx = jnp.dot(p_basis, q_factor.T, precision=lax.Precision.HIGHEST)
    new_error = (merged_all - approx[None]).astype(jnp.bfloat16).reshape(N_DP * D, F)
    return (new_error, p_basis, q_factor)
```

```python
import jax
import jax.numpy as jnp
from jax import lax
from jax.sharding import PartitionSpec as P

AXES = ("dp", "mp")
HIGH = lax.Precision.HIGHEST


class Layout:
    def __init__(self, n_dp, n_mp):
        self.core = 2 if n_dp % 2 == 0 else 1
        self.side = 2 if n_dp % 4 == 0 else 1
        self.ring = n_dp // (self.core * self.side)
        self.mp = n_mp
        self.plane = self.side * n_mp

    def index(self, z, x, c, y):
        return ((z * self.side + x) * self.core + c) * self.mp + y

    def perm(self, move):
        pairs = []
        for z in range(self.ring):
            for x in range(self.side):
                for c in range(self.core):
                    for y in range(self.mp):
                        pairs.append((self.index(z, x, c, y), self.index(*move(z, x, c, y))))
        return pairs

    def core_perm(self):
        return self.perm(lambda z, x, c, y: (z, x, c ^ 1, y))

    def side_perm(self):
        return self.perm(lambda z, x, c, y: (z, x ^ 1, c, y))

    def plane_perm(self, j):
        def move(z, x, c, y):
            w = (x * self.mp + y) ^ j
            return z, w // self.mp, c, w % self.mp

        return self.perm(move)

    def ring_perm(self, j):
        return self.perm(lambda z, x, c, y: (z ^ j, x, c, y))


def send(value, perm):
    return lax.ppermute(value, AXES, perm)


def tree(parts):
    while len(parts) > 1:
        parts = [parts[i] + parts[i + 1] for i in range(0, len(parts), 2)]
    return parts[0]


def ring_sum(lay, value):
    return tree([value] + [send(value, lay.ring_perm(j)) for j in range(1, lay.ring)])


def sum_p(lay, parts):
    half = parts[0] + send(parts[1], lay.core_perm())
    block = half[0]
    for j in range(1, lay.plane):
        block = block + send(half[j], lay.plane_perm(j))
    block = ring_sum(lay, block)
    half = jnp.stack([block] + [send(block, lay.plane_perm(j)) for j in range(1, lay.plane)])
    return jnp.stack([half, send(half, lay.core_perm())])


def sum_q(lay, parts):
    half = parts[0] + send(parts[1], lay.core_perm())
    half = half + send(half, lay.side_perm())
    half = ring_sum(lay, half)
    return jnp.stack([half, send(half, lay.core_perm())])


def relative(array, axis, own):
    n = array.shape[axis]
    return jnp.stack([lax.dynamic_index_in_dim(array, own ^ j, axis, keepdims=False) for j in range(n)])


def body(activations, out_grads, error_memory, q_previous):
    n_dp = lax.axis_size("dp")
    lay = Layout(n_dp, lax.axis_size("mp"))
    width = activations.shape[2]
    rank = q_previous.shape[1]
    columns = out_grads.shape[2]
    token_rows = activations.reshape(-1, width)
    grad_rows = out_grads.reshape(-1, columns)
    dp, mp = lax.axis_index("dp"), lax.axis_index("mp")
    core = dp % lay.core
    plane = (dp // lay.core % lay.side) * lay.mp + mp

    projected = jnp.dot(grad_rows, q_previous, precision=HIGH)
    p_partial = jnp.einsum(
        "td,tr->rd", token_rows, projected, precision=HIGH, preferred_element_type=jnp.float32
    ) + jnp.einsum("df,fr->rd", error_memory, q_previous, precision=HIGH, preferred_element_type=jnp.float32)
    merged = jnp.einsum(
        "td,tf->df", token_rows, grad_rows, preferred_element_type=jnp.float32
    ) + error_memory.astype(jnp.float32)

    lanes = -(-width // (128 * lay.core)) * 128
    padded = jnp.pad(p_partial, ((0, 0), (0, lanes * lay.core - width)))
    blocks = padded.reshape(lay.plane, rank // lay.plane, lay.core, lanes).transpose(2, 0, 1, 3)
    p_blocks = sum_p(lay, relative(relative(blocks, 0, core), 1, plane).transpose(1, 0, 2, 3))
    blocks = relative(relative(p_blocks, 0, core), 1, plane).transpose(1, 0, 2, 3)
    p_whole = blocks.transpose(1, 2, 0, 3).reshape(rank, -1)[:, :width]

    q_partial = jnp.einsum("rd,df->rf", p_whole, merged, precision=HIGH)
    q_halves = q_partial.reshape(lay.core, rank // lay.core, columns)
    q_sum = relative(sum_q(lay, relative(q_halves, 0, core)), 0, core).reshape(rank, columns)

    gram = jnp.dot(p_whole, p_whole.T, precision=HIGH)
    lower = jnp.linalg.cholesky(gram)
    inverse = jax.scipy.linalg.solve_triangular(lower, jnp.eye(rank, dtype=jnp.float32), lower=True)
    p_basis = jnp.dot(inverse, p_whole, precision=HIGH)
    block_rows = width // n_dp
    share = lax.dynamic_slice_in_dim(p_basis, dp * block_rows, block_rows, 1).T
    q_factor = jnp.dot(inverse, q_sum, precision=HIGH) / n_dp
    approx = jnp.einsum("rd,rf->df", p_basis, q_factor, precision=HIGH)
    new_error = (merged - approx).astype(jnp.bfloat16)
    return (new_error, share, q_factor.T)


def solution(mesh):
    in_specs = (P(None, "dp", None), P(None, "dp", "mp"), P("dp", "mp"), P("mp", None))
    out_specs = (P("dp", "mp"), P("dp", None), P("mp", None))
    return jax.shard_map(body, mesh=mesh, in_specs=in_specs, out_specs=out_specs, check_vma=False)
```

```python
import jax
import jax.numpy as jnp
from jax import lax
from jax.experimental import pallas as pl
from jax.experimental.pallas import tpu as pltpu
from jax.sharding import PartitionSpec as P

AXES = ("dp", "mp")
HIGH = lax.Precision.HIGHEST


class Layout:
    def __init__(self, n_dp, n_mp):
        self.core = 2 if n_dp % 2 == 0 else 1
        self.side = 2 if n_dp % 4 == 0 else 1
        self.ring = n_dp // (self.core * self.side)
        self.mp = n_mp
        self.plane = self.side * n_mp

    def index(self, z, x, c, y):
        return ((z * self.side + x) * self.core + c) * self.mp + y

    def perm(self, move):
        pairs = []
        for z in range(self.ring):
            for x in range(self.side):
                for c in range(self.core):
                    for y in range(self.mp):
                        pairs.append((self.index(z, x, c, y), self.index(*move(z, x, c, y))))
        return pairs

    def core_perm(self):
        return self.perm(lambda z, x, c, y: (z, x, c ^ 1, y))

    def side_perm(self):
        return self.perm(lambda z, x, c, y: (z, x ^ 1, c, y))

    def plane_perm(self, j):
        def move(z, x, c, y):
            w = (x * self.mp + y) ^ j
            return z, w // self.mp, c, w % self.mp

        return self.perm(move)

    def ring_perm(self, j):
        return self.perm(lambda z, x, c, y: (z ^ j, x, c, y))


def send(value, perm):
    return lax.ppermute(value, AXES, perm)


def tree(parts):
    while len(parts) > 1:
        parts = [parts[i] + parts[i + 1] for i in range(0, len(parts), 2)]
    return parts[0]


def ring_sum(lay, value):
    return tree([value] + [send(value, lay.ring_perm(j)) for j in range(1, lay.ring)])


def sum_p(lay, own, other):
    half = own + send(other, lay.core_perm()) if lay.core > 1 else own
    block = half[0]
    for j in range(1, lay.plane):
        block = block + send(half[j], lay.plane_perm(j))
    block = ring_sum(lay, block)
    half = jnp.stack([block] + [send(block, lay.plane_perm(j)) for j in range(1, lay.plane)])
    return half, send(half, lay.core_perm()) if lay.core > 1 else half


def sum_q(lay, own, other):
    half = own + send(other, lay.core_perm()) if lay.core > 1 else own
    if lay.side > 1:
        half = half + send(half, lay.side_perm())
    half = ring_sum(lay, half)
    return half, send(half, lay.core_perm()) if lay.core > 1 else half


def pieces(value):
    high = value.astype(jnp.bfloat16)
    rest = value - high.astype(jnp.float32)
    middle = rest.astype(jnp.bfloat16)
    low = (rest - middle.astype(jnp.float32)).astype(jnp.bfloat16)
    return high, middle, low


def stacked(value):
    return jnp.concatenate(pieces(value), axis=0)


def folded(value):
    third = value.shape[0] // 3
    return value[:third] + value[third : 2 * third] + value[2 * third :]


def dot(a, b, dims, precision=None):
    return lax.dot_general(
        a, b, ((dims[0], dims[1]), ((), ())), precision=precision, preferred_element_type=jnp.float32
    )


NN = ((1,), (0,))
NT = ((1,), (1,))


def chunks(width, lanes, step):
    found = []
    for half in range(-(-width // lanes)):
        end = min(lanes, width - half * lanes)
        for offset in range(0, end, step):
            found.append((half, offset, half * lanes + offset, min(step, end - offset)))
    return found


def vmem():
    return pl.BlockSpec(memory_space=pltpu.VMEM)


def smem():
    return pl.BlockSpec(memory_space=pltpu.SMEM)


def hbm():
    return pl.BlockSpec(memory_space=pltpu.HBM)


def params(mib):
    return pltpu.CompilerParams(vmem_limit_bytes=mib << 20)


def fetch(source, target, sems, row, cuts):
    copies = []
    for i, (_, _, start, size) in enumerate(cuts):
        where = (slice(None), pl.ds(start, size))
        copies.append(pltpu.make_async_copy(source.at[where], target.at[where], sems.at[row, i]))
    return copies


def p_kernel(lay, cuts, place, q_ref, g_ref, a_hbm, e_hbm, own_ref, other_ref, a_buf, e_buf, sems):
    copies = list(zip(fetch(e_hbm, e_buf, sems, 0, cuts), fetch(a_hbm, a_buf, sems, 1, cuts)))
    for e_copy, a_copy in copies:
        e_copy.start()
        a_copy.start()
    core, plane = place[0], place[1]
    rank = q_ref.shape[0]
    rows = rank // lay.plane
    lanes = own_ref.shape[2]
    tail = lanes * lay.core - cuts[-1][2] - cuts[-1][3]
    q3 = stacked(q_ref[...])
    h3 = stacked(jnp.concatenate([folded(dot(q3, g_ref[m], NN)) for m in range(g_ref.shape[0])], axis=1))
    for (half, offset, start, size), (e_copy, a_copy) in zip(cuts, copies):
        e_copy.wait()
        a_copy.wait()
        part = dot(q3, e_buf[:, pl.ds(start, size)], NN) + dot(h3, a_buf[:, pl.ds(start, size)], NN)
        part = folded(part)

        def store(ref, part=part, offset=offset, size=size):
            for b in range(lay.plane):
                ref[plane ^ b, :, pl.ds(offset, size)] = part[b * rows : (b + 1) * rows]

        if lay.core == 1:
            store(own_ref)
        else:
            pl.when(core == half)(lambda: store(own_ref))
            pl.when(core != half)(lambda: store(other_ref))
    if tail:
        zero = jnp.zeros((lay.plane, rows, tail), jnp.float32)

        @pl.when(core == lay.core - 1)
        def _():
            own_ref[:, :, pl.ds(lanes - tail, tail)] = zero

        @pl.when(core != lay.core - 1)
        def _():
            other_ref[:, :, pl.ds(lanes - tail, tail)] = zero


def q_kernel(lay, cuts, place, own_ref, other_ref, g_ref, a_ref, e_ref, p_ref, gram_ref, mine_ref, their_ref):
    core, plane = place[0], place[1]
    total = t3 = gram = None
    for half, offset, start, size in cuts:

        def load(ref):
            return jnp.concatenate([ref[plane ^ b, :, pl.ds(offset, size)] for b in range(lay.plane)], axis=0)

        part = load(own_ref)
        if lay.core > 1:
            part = jnp.where(core == half, part, load(other_ref))
        p_ref[:, pl.ds(start, size)] = part
        p3 = stacked(part)
        q_term = dot(p3, e_ref[:, pl.ds(start, size)], NT)
        t_term = dot(p3, a_ref[:, pl.ds(start, size)], NT)
        g_term = dot(p3, p3, NT)
        total = q_term if total is None else total + q_term
        t3 = t_term if t3 is None else t3 + t_term
        gram = g_term if gram is None else gram + g_term
    t3 = stacked(folded(t3))
    batch = g_ref.shape[2]
    for m in range(g_ref.shape[0]):
        total = total + dot(t3[:, m * batch : (m + 1) * batch], g_ref[m], NT)
    total = folded(total)
    rank = total.shape[0]
    gram = folded(gram)
    gram_ref[...] = gram[:, :rank] + gram[:, rank : 2 * rank] + gram[:, 2 * rank :]
    rows = rank // lay.core
    if lay.core == 1:
        mine_ref[...] = total
        their_ref[...] = total
    else:
        low, high = total[:rows], total[rows:]
        mine_ref[...] = jnp.where(core == 0, low, high)
        their_ref[...] = jnp.where(core == 0, high, low)


def inverse_kernel(gram_ref, inverse_ref):
    rank = gram_ref.shape[0]
    row = lax.broadcasted_iota(jnp.int32, (rank, 2 * rank), 0)
    column = lax.broadcasted_iota(jnp.int32, (rank, 2 * rank), 1)
    unit = jnp.where(column - rank == row, 1.0, 0.0).astype(jnp.float32)
    work = jnp.where(column < rank, jnp.concatenate([gram_ref[...], gram_ref[...]], axis=1), unit)
    for k in range(rank):
        pivot = work[k : k + 1]
        scale = 1.0 / jnp.sqrt(pivot[:, k : k + 1])
        scaled = pivot * scale
        factor = work[:, k : k + 1] * scale
        work = jnp.where(row > k, work - factor * scaled, jnp.where(row == k, scaled, work))
    inverse_ref[...] = work[:, rank:]


def basis_kernel(cuts, inverse_ref, p_ref, basis_ref, split_ref):
    for _, _, start, size in cuts:
        part = dot(inverse_ref[...], p_ref[:, pl.ds(start, size)], NN, HIGH)
        basis_ref[:, pl.ds(start, size)] = part
        high, middle, _ = pieces(part)
        split_ref[:, pl.ds(start, size)] = jnp.concatenate([high, middle, high], axis=0)


def error_kernel(
    lay, cuts, n_dp, place, mine_ref, their_ref, inverse_ref, split_ref, g_ref, a_ref, e_ref, o_hbm, q_ref, o_buf, sems
):
    core = place[0]
    if lay.core == 1:
        q_sum = mine_ref[...]
    else:
        mine, theirs = mine_ref[...], their_ref[...]
        q_sum = jnp.concatenate(
            [jnp.where(core == 0, mine, theirs), jnp.where(core == 0, theirs, mine)], axis=0
        )
    factor = dot(inverse_ref[...], q_sum, NN, HIGH) / n_dp
    q_ref[...] = factor
    high, middle, _ = [piece.astype(jnp.float32) for piece in pieces(factor)]
    left = jnp.concatenate([high, high, middle], axis=0).T.astype(jnp.bfloat16)
    grads = jnp.concatenate([g_ref[m] for m in range(g_ref.shape[0])], axis=1)
    out = fetch(o_buf, o_hbm, sems, 0, cuts)
    for (_, _, start, size), o_copy in zip(cuts, out):
        where = (slice(None), pl.ds(start, size))
        merged = dot(grads, a_ref[where], NN) + e_ref[where].astype(jnp.float32)
        o_buf[where] = (merged - dot(left, split_ref[where], NN)).astype(jnp.bfloat16)
        o_copy.start()
    for o_copy in out:
        o_copy.wait()


def body(activations, out_grads, error_memory, q_previous):
    n_dp = lax.axis_size("dp")
    lay = Layout(n_dp, lax.axis_size("mp"))
    width = activations.shape[2]
    columns, rank = q_previous.shape
    acts = activations.reshape(-1, width)
    grads, memory, previous = out_grads.transpose(0, 2, 1), error_memory.T, q_previous.T
    tokens = acts.shape[0]
    dp, mp = lax.axis_index("dp"), lax.axis_index("mp")
    place = jnp.stack([dp % lay.core, (dp // lay.core % lay.side) * lay.mp + mp]).astype(jnp.int32)
    f32, bf16 = jnp.float32, jnp.bfloat16

    lanes = -(-width // (128 * lay.core)) * 128
    rows = rank // lay.plane
    cuts = chunks(width, lanes, 512)
    buffers = [pltpu.VMEM((tokens, width), bf16), pltpu.VMEM((columns, width), bf16)]
    half = jax.ShapeDtypeStruct((lay.plane, rows, lanes), f32)
    own, other = pl.pallas_call(
        lambda *refs: p_kernel(lay, cuts, *refs),
        out_shape=(half, half),
        in_specs=[smem(), vmem(), vmem(), hbm(), hbm()],
        out_specs=(vmem(), vmem()),
        scratch_shapes=buffers + [pltpu.SemaphoreType.DMA((2, len(cuts)))],
        compiler_params=params(24),
        name="p_partial",
    )(
        place,
        previous,
        grads,
        pltpu.with_memory_space_constraint(acts, pltpu.HBM),
        pltpu.with_memory_space_constraint(memory, pltpu.HBM),
    )

    own, other = sum_p(lay, own, other)
    q_half = jax.ShapeDtypeStruct((rank // lay.core, columns), f32)
    p_whole, gram, mine, theirs = pl.pallas_call(
        lambda *refs: q_kernel(lay, cuts, *refs),
        out_shape=(
            jax.ShapeDtypeStruct((rank, width), f32),
            jax.ShapeDtypeStruct((rank, rank), f32),
            q_half,
            q_half,
        ),
        in_specs=[smem()] + [vmem()] * 5,
        out_specs=(vmem(),) * 4,
        compiler_params=params(24),
        name="q_partial",
    )(place, own, other, grads, acts, memory)

    inverse = pl.pallas_call(
        inverse_kernel,
        out_shape=jax.ShapeDtypeStruct((rank, rank), f32),
        in_specs=[vmem()],
        out_specs=vmem(),
        compiler_params=params(4),
        name="inverse",
    )(gram)
    basis, split = pl.pallas_call(
        lambda *refs: basis_kernel(cuts, *refs),
        out_shape=(jax.ShapeDtypeStruct((rank, width), f32), jax.ShapeDtypeStruct((3 * rank, width), bf16)),
        in_specs=[vmem()] * 2,
        out_specs=(vmem(),) * 2,
        compiler_params=params(8),
        name="basis",
    )(inverse, p_whole)
    block_rows = width // n_dp
    share = lax.dynamic_slice_in_dim(basis, dp * block_rows, block_rows, 1).T

    mine, theirs = sum_q(lay, mine, theirs)

    new_error, q_factor = pl.pallas_call(
        lambda *refs: error_kernel(lay, cuts, n_dp, *refs),
        out_shape=(jax.ShapeDtypeStruct((columns, width), bf16), jax.ShapeDtypeStruct((rank, columns), f32)),
        in_specs=[smem()] + [vmem()] * 7,
        out_specs=(hbm(), vmem()),
        scratch_shapes=[buffers[1], pltpu.SemaphoreType.DMA((1, len(cuts)))],
        compiler_params=params(24),
        name="new_error",
    )(place, mine, theirs, inverse, split, grads, acts, memory)
    return (new_error.T, share, q_factor.T)


def solution(mesh):
    in_specs = (P(None, "dp", None), P(None, "dp", "mp"), P("dp", "mp"), P("mp", None))
    out_specs = (P("dp", "mp"), P("dp", None), P("mp", None))
    return jax.shard_map(body, mesh=mesh, in_specs=in_specs, out_specs=out_specs, check_vma=False)
```

```python
import jax
import jax.numpy as jnp
from jax import lax
from jax.experimental import pallas as pl
from jax.experimental.pallas import tpu as pltpu
from jax.sharding import PartitionSpec as P

AXES = ("dp", "mp")
HIGH = lax.Precision.HIGHEST


class Layout:
    def __init__(self, n_dp, n_mp):
        self.core = 2 if n_dp % 2 == 0 else 1
        self.side = 2 if n_dp % 4 == 0 else 1
        self.ring = n_dp // (self.core * self.side)
        self.mp = n_mp
        self.plane = self.side * n_mp

    def index(self, z, x, c, y):
        return ((z * self.side + x) * self.core + c) * self.mp + y

    def perm(self, move):
        pairs = []
        for z in range(self.ring):
            for x in range(self.side):
                for c in range(self.core):
                    for y in range(self.mp):
                        pairs.append((self.index(z, x, c, y), self.index(*move(z, x, c, y))))
        return pairs

    def core_perm(self):
        return self.perm(lambda z, x, c, y: (z, x, c ^ 1, y))

    def side_perm(self):
        return self.perm(lambda z, x, c, y: (z, x ^ 1, c, y))

    def plane_perm(self, j):
        def move(z, x, c, y):
            w = (x * self.mp + y) ^ j
            return z, w // self.mp, c, w % self.mp

        return self.perm(move)

    def ring_perm(self, j):
        return self.perm(lambda z, x, c, y: (z ^ j, x, c, y))


def send(value, perm):
    return lax.ppermute(value, AXES, perm)


def tree(parts):
    while len(parts) > 1:
        parts = [parts[i] + parts[i + 1] for i in range(0, len(parts), 2)]
    return parts[0]


def ring_sum(lay, value):
    return tree([value] + [send(value, lay.ring_perm(j)) for j in range(1, lay.ring)])


def sum_p(lay, own, other):
    half = own + send(other, lay.core_perm()) if lay.core > 1 else own
    block = half[0]
    for j in range(1, lay.plane):
        block = block + send(half[j], lay.plane_perm(j))
    block = ring_sum(lay, block)
    half = jnp.stack([block] + [send(block, lay.plane_perm(j)) for j in range(1, lay.plane)])
    return half, send(half, lay.core_perm()) if lay.core > 1 else half


def sum_q(lay, own, other):
    half = own + send(other, lay.core_perm()) if lay.core > 1 else own
    if lay.side > 1:
        half = half + send(half, lay.side_perm())
    half = ring_sum(lay, half)
    return half, send(half, lay.core_perm()) if lay.core > 1 else half


def pieces(value):
    high = value.astype(jnp.bfloat16)
    rest = value - high.astype(jnp.float32)
    middle = rest.astype(jnp.bfloat16)
    low = (rest - middle.astype(jnp.float32)).astype(jnp.bfloat16)
    return high, middle, low


def stacked(value):
    return jnp.concatenate(pieces(value), axis=0)


def folded(value):
    third = value.shape[0] // 3
    return value[:third] + value[third : 2 * third] + value[2 * third :]


def dot(a, b, dims, precision=None):
    return lax.dot_general(
        a, b, ((dims[0], dims[1]), ((), ())), precision=precision, preferred_element_type=jnp.float32
    )


NN = ((1,), (0,))
NT = ((1,), (1,))


def chunks(width, lanes, step):
    found = []
    for half in range(-(-width // lanes)):
        end = min(lanes, width - half * lanes)
        for offset in range(0, end, step):
            found.append((half, offset, half * lanes + offset, min(step, end - offset)))
    return found


def vmem():
    return pl.BlockSpec(memory_space=pltpu.VMEM)


def smem():
    return pl.BlockSpec(memory_space=pltpu.SMEM)


def hbm():
    return pl.BlockSpec(memory_space=pltpu.HBM)


def params(mib):
    return pltpu.CompilerParams(vmem_limit_bytes=mib << 20)


def fetch(source, target, sems, row, cuts):
    copies = []
    for i, (_, _, start, size) in enumerate(cuts):
        where = (slice(None), pl.ds(start, size))
        copies.append(pltpu.make_async_copy(source.at[where], target.at[where], sems.at[row, i]))
    return copies


def p_kernel(
    lay, cuts, place, q_hbm, g_hbm, a_hbm, e_hbm, own_ref, other_ref, g_ref, a_ref, e_ref, q_ref, sems, small_sems
):
    small = [
        pltpu.make_async_copy(q_hbm, q_ref, small_sems.at[0]),
        pltpu.make_async_copy(g_hbm, g_ref, small_sems.at[1]),
    ]
    copies = list(zip(fetch(e_hbm, e_ref, sems, 0, cuts), fetch(a_hbm, a_ref, sems, 1, cuts)))
    for pair in [small] + copies:
        for copy in pair:
            copy.start()
    for copy in small:
        copy.wait()
    core, plane = place[0], place[1]
    rank = q_ref.shape[0]
    rows = rank // lay.plane
    lanes = own_ref.shape[2]
    tail = lanes * lay.core - cuts[-1][2] - cuts[-1][3]
    q3 = stacked(q_ref[...])
    h3 = stacked(jnp.concatenate([folded(dot(q3, g_ref[m], NN)) for m in range(g_ref.shape[0])], axis=1))
    for (half, offset, start, size), (e_copy, a_copy) in zip(cuts, copies):
        e_copy.wait()
        a_copy.wait()
        part = dot(q3, e_ref[:, pl.ds(start, size)], NN) + dot(h3, a_ref[:, pl.ds(start, size)], NN)
        part = folded(part)

        def store(ref, part=part, offset=offset, size=size):
            for b in range(lay.plane):
                ref[plane ^ b, :, pl.ds(offset, size)] = part[b * rows : (b + 1) * rows]

        if lay.core == 1:
            store(own_ref)
        else:
            pl.when(core == half)(lambda: store(own_ref))
            pl.when(core != half)(lambda: store(other_ref))
    if tail:
        zero = jnp.zeros((lay.plane, rows, tail), jnp.float32)

        @pl.when(core == lay.core - 1)
        def _():
            own_ref[:, :, pl.ds(lanes - tail, tail)] = zero

        @pl.when(core != lay.core - 1)
        def _():
            other_ref[:, :, pl.ds(lanes - tail, tail)] = zero


def q_kernel(lay, cuts, place, own_ref, other_ref, g_ref, a_ref, e_ref, p_ref, gram_ref, mine_ref, their_ref):
    core, plane = place[0], place[1]
    total = t3 = gram = None
    for half, offset, start, size in cuts:

        def load(ref):
            return jnp.concatenate([ref[plane ^ b, :, pl.ds(offset, size)] for b in range(lay.plane)], axis=0)

        part = load(own_ref)
        if lay.core > 1:
            part = jnp.where(core == half, part, load(other_ref))
        p_ref[:, pl.ds(start, size)] = part
        p3 = stacked(part)
        q_term = dot(p3, e_ref[:, pl.ds(start, size)], NT)
        t_term = dot(p3, a_ref[:, pl.ds(start, size)], NT)
        g_term = dot(p3, p3, NT)
        total = q_term if total is None else total + q_term
        t3 = t_term if t3 is None else t3 + t_term
        gram = g_term if gram is None else gram + g_term
    t3 = stacked(folded(t3))
    batch = g_ref.shape[2]
    for m in range(g_ref.shape[0]):
        total = total + dot(t3[:, m * batch : (m + 1) * batch], g_ref[m], NT)
    total = folded(total)
    rank = total.shape[0]
    gram = folded(gram)
    gram_ref[...] = gram[:, :rank] + gram[:, rank : 2 * rank] + gram[:, 2 * rank :]
    rows = rank // lay.core
    if lay.core == 1:
        mine_ref[...] = total
        their_ref[...] = total
    else:
        low, high = total[:rows], total[rows:]
        mine_ref[...] = jnp.where(core == 0, low, high)
        their_ref[...] = jnp.where(core == 0, high, low)


def inverse_kernel(gram_ref, inverse_ref):
    rank = gram_ref.shape[0]
    row = lax.broadcasted_iota(jnp.int32, (rank, 2 * rank), 0)
    column = lax.broadcasted_iota(jnp.int32, (rank, 2 * rank), 1)
    unit = jnp.where(column - rank == row, 1.0, 0.0).astype(jnp.float32)
    work = jnp.where(column < rank, jnp.concatenate([gram_ref[...], gram_ref[...]], axis=1), unit)
    for k in range(rank):
        pivot = work[k : k + 1]
        scale = 1.0 / jnp.sqrt(pivot[:, k : k + 1])
        scaled = pivot * scale
        factor = work[:, k : k + 1] * scale
        work = jnp.where(row > k, work - factor * scaled, jnp.where(row == k, scaled, work))
    inverse_ref[...] = work[:, rank:]


def basis_kernel(cuts, place, inverse_ref, p_ref, share_ref, split_ref, basis):
    for _, _, start, size in cuts:
        part = dot(inverse_ref[...], p_ref[:, pl.ds(start, size)], NN, HIGH)
        basis[:, pl.ds(start, size)] = part
        high, middle, _ = pieces(part)
        split_ref[:, pl.ds(start, size)] = jnp.concatenate([high, middle, high], axis=0)
    first = place[2]
    window = share_window(share_ref.shape[1])
    held = basis[:, pl.ds(pl.multiple_of(first // 128 * 128, 128), window)]
    share_ref[...] = pltpu.roll(held, (window - first % 128) % window, 1)[:, : share_ref.shape[1]]


def share_window(block):
    return -(-(block + 127) // 128) * 128


def error_kernel(
    lay, cuts, n_dp, place, mine_ref, their_ref, inverse_ref, split_ref, g_ref, a_ref, e_ref, o_hbm, q_ref, o_buf, sems
):
    core = place[0]
    if lay.core == 1:
        q_sum = mine_ref[...]
    else:
        mine, theirs = mine_ref[...], their_ref[...]
        q_sum = jnp.concatenate(
            [jnp.where(core == 0, mine, theirs), jnp.where(core == 0, theirs, mine)], axis=0
        )
    factor = dot(inverse_ref[...], q_sum, NN, HIGH) / n_dp
    q_ref[...] = factor
    high, middle, _ = [piece.astype(jnp.float32) for piece in pieces(factor)]
    left = jnp.concatenate([high, high, middle], axis=0).T.astype(jnp.bfloat16)
    grads = jnp.concatenate([g_ref[m] for m in range(g_ref.shape[0])], axis=1)
    out = fetch(o_buf, o_hbm, sems, 0, cuts)
    for (_, _, start, size), o_copy in zip(cuts, out):
        where = (slice(None), pl.ds(start, size))
        merged = dot(grads, a_ref[where], NN) + e_ref[where].astype(jnp.float32)
        o_buf[where] = (merged - dot(left, split_ref[where], NN)).astype(jnp.bfloat16)
        o_copy.start()
    for o_copy in out:
        o_copy.wait()


def body(activations, out_grads, error_memory, q_previous):
    n_dp = lax.axis_size("dp")
    lay = Layout(n_dp, lax.axis_size("mp"))
    width = activations.shape[2]
    columns, rank = q_previous.shape
    acts = activations.reshape(-1, width)
    grads, memory, previous = out_grads.transpose(0, 2, 1), error_memory.T, q_previous.T
    dp, mp = lax.axis_index("dp"), lax.axis_index("mp")
    block_rows = width // n_dp
    plane = (dp // lay.core % lay.side) * lay.mp + mp
    place = jnp.stack([dp % lay.core, plane, dp * block_rows]).astype(jnp.int32)
    f32, bf16 = jnp.float32, jnp.bfloat16

    lanes = -(-width // (128 * lay.core)) * 128
    rows = rank // lay.plane
    cuts = chunks(width, lanes, 512)
    half = jax.ShapeDtypeStruct((lay.plane, rows, lanes), f32)
    own, other, grads, acts, memory = pl.pallas_call(
        lambda *refs: p_kernel(lay, cuts, *refs),
        out_shape=(half, half) + tuple(pltpu.VMEM(x.shape, bf16) for x in (grads, acts, memory)),
        in_specs=[smem()] + [hbm()] * 4,
        out_specs=(vmem(),) * 5,
        scratch_shapes=[
            pltpu.VMEM(previous.shape, f32),
            pltpu.SemaphoreType.DMA((2, len(cuts))),
            pltpu.SemaphoreType.DMA((2,)),
        ],
        compiler_params=params(16),
        name="p_partial",
    )(place, *[pltpu.with_memory_space_constraint(x, pltpu.HBM) for x in (previous, grads, acts, memory)])
    grads, acts, memory = [pltpu.with_memory_space_constraint(x, pltpu.VMEM) for x in (grads, acts, memory)]

    own, other = sum_p(lay, own, other)
    q_half = jax.ShapeDtypeStruct((rank // lay.core, columns), f32)
    p_whole, gram, mine, theirs = pl.pallas_call(
        lambda *refs: q_kernel(lay, cuts, *refs),
        out_shape=(
            jax.ShapeDtypeStruct((rank, width), f32),
            jax.ShapeDtypeStruct((rank, rank), f32),
            q_half,
            q_half,
        ),
        in_specs=[smem()] + [vmem()] * 5,
        out_specs=(vmem(),) * 4,
        compiler_params=params(24),
        name="q_partial",
    )(place, own, other, grads, acts, memory)

    inverse = pl.pallas_call(
        inverse_kernel,
        out_shape=jax.ShapeDtypeStruct((rank, rank), f32),
        in_specs=[vmem()],
        out_specs=vmem(),
        compiler_params=params(4),
        name="inverse",
    )(gram)
    share, split = pl.pallas_call(
        lambda *refs: basis_kernel(cuts, *refs),
        out_shape=(jax.ShapeDtypeStruct((rank, block_rows), f32), jax.ShapeDtypeStruct((3 * rank, width), bf16)),
        in_specs=[smem()] + [vmem()] * 2,
        out_specs=(vmem(),) * 2,
        scratch_shapes=[pltpu.VMEM((rank, lanes * lay.core + share_window(block_rows)), f32)],
        compiler_params=params(8),
        name="basis",
    )(place, inverse, p_whole)

    mine, theirs = sum_q(lay, mine, theirs)

    new_error, q_factor = pl.pallas_call(
        lambda *refs: error_kernel(lay, cuts, n_dp, *refs),
        out_shape=(jax.ShapeDtypeStruct((columns, width), bf16), jax.ShapeDtypeStruct((rank, columns), f32)),
        in_specs=[smem()] + [vmem()] * 7,
        out_specs=(hbm(), vmem()),
        scratch_shapes=[pltpu.VMEM((columns, width), bf16), pltpu.SemaphoreType.DMA((1, len(cuts)))],
        compiler_params=params(24),
        name="new_error",
    )(place, mine, theirs, inverse, split, grads, acts, memory)
    return (new_error.T, share.T, q_factor.T)


def solution(mesh):
    in_specs = (P(None, "dp", None), P(None, "dp", "mp"), P("dp", "mp"), P("mp", None))
    out_specs = (P("dp", "mp"), P("dp", None), P("mp", None))
    return jax.shard_map(body, mesh=mesh, in_specs=in_specs, out_specs=out_specs, check_vma=False)
```
